32 devices in a mesh: seq: 32 (over z, y, x, core), chan: 1.
Axes of the slice: x: 2, y: 2, z: 4, core: 2. Of those that a mesh axis runs over, the one named last changes fastest.
Arguments:
- proj_in: bfloat16 [5120, 3, 8192], P('seq', None, 'chan'), may hold values from -6 to 6
- short_taps: float32 [7, 3, 8192], P(None, None, 'chan'), may hold values from -2.4 to 2.4
- long_taps: float32 [128, 8192], P(None, 'chan'), may hold values from -0.5 to 0.5
- skip_gain: float32 [8192], P('chan'), may hold values from -1 to 1
- keep: int32 [8192], P('chan'), may hold values from 0 to 1, as said below
- w_out: bfloat16 [8192, 4096], P('chan', 'seq'), may hold values from -0.09375 to 0.09375
- grad_out: bfloat16 [5120, 4096], P('seq', 'chan'), may hold values from -6 to 6
Outputs:
- output: bfloat16 [5120, 4096], P('seq', 'chan')
- grad_proj_in: bfloat16 [5120, 3, 8192], P('seq', None, 'chan')
- grad_long_taps: float32 [128, 8192], P(None, 'chan')
- grad_short_taps: float32 [7, 3, 8192], P(None, None, 'chan')
- grad_skip_gain: float32 [8192], P('chan')
The draws below stay inside these ranges and needn't reach their ends.
Inputs may be any that keep to these rules, and one draw needn't show every extreme that they name: `keep`: in every aligned group of 16 consecutive channels exactly half of the entries are 1 and the rest 0.
All inputs are finite; a program needn't handle non-finite values.
Results may differ from the reference program's by a relative error of at most 0.012.
Values may be sent and summed in bfloat16 or wider, within the bound.
A program may use at most 192 MiB of HBM per device.

```python
import jax
import jax.numpy as jnp
from jax import lax

D = 8192
DOUT = 4096
TAPS = 128
SHORT = 7
GROUP = 16
TOKENS = 5120
CHAN_BLOCK = 8192
N_CHAN = 1


def draw_keep(key, part):
    order = jax.random.permutation(key, D).reshape(D // GROUP, GROUP)
    ranks = jnp.argsort(jnp.argsort(order, axis=1, stable=True), axis=1, stable=True)
    return (ranks < GROUP // 2).astype(jnp.int32).reshape(D)


def steps_of(key, extent, cuts, smallest, high):
    def one(position, shards_of):
        draws = jax.random.uniform(jax.random.fold_in(jax.random.fold_in(key, 6), position), (shards_of,), jnp.float32, smallest / len(cuts), high / len(cuts))
        return jnp.repeat(jnp.exp(draws), extent[position] // shards_of).reshape((-1,) + (1,) * (len(extent) - position - 1))

    gain = one(*cuts[0])
    for cut in cuts[1:]:
        gain = gain * one(*cut)
    return gain


def gaussian(own_key, extent, width, reach, pieces=(), kind=jnp.bfloat16):
    loudness = steps_of(own_key, extent, pieces, -0.22, 0.18) if pieces else 1.0
    drawn = jax.random.normal(own_key, extent, jnp.float32) * width * loudness
    return jnp.minimum(jnp.maximum(drawn, -reach), reach).astype(kind)


def setup_inputs(seed: int = 0) -> dict:
    streams_of = jax.random.split(jax.random.key(seed), 8)
    return {
        "proj_in": gaussian(streams_of[0], (TOKENS, 3, D), 1.0, 6.0, ((0, 32),)),
        "short_taps": gaussian(streams_of[1], (SHORT, 3, D), 0.4, 2.4, (), jnp.float32),
        "long_taps": gaussian(streams_of[2], (TAPS, D), TAPS ** -0.5, 0.5, (), jnp.float32),
        "skip_gain": jnp.clip(jax.random.uniform(streams_of[3], (D,), jnp.float32, -1.0, 1.0), -1.0, 1.0),
        "keep": draw_keep(jax.random.fold_in(streams_of[7], 71), 0),
        "w_out": gaussian(streams_of[5], (D, DOUT), (D // 2) ** -0.5, 0.09375, ((1, 32),)),
        "grad_out": gaussian(streams_of[6], (TOKENS, DOUT), 1.0, 6.0, ((0, 32),)),
    }


def shift_down(values, steps):
    if steps == 0:
        return values
    zero_rows = jnp.zeros((steps,) + values.shape[1:], values.dtype)
    return jnp.concatenate([zero_rows, values[:-steps]], axis=0)


def shift_up(values, steps):
    if steps == 0:
        return values
    zero_rows = jnp.zeros((steps,) + values.shape[1:], values.dtype)
    return jnp.concatenate([values[steps:], zero_rows], axis=0)


def causal_long(signal, filt):
    length = 2 * signal.shape[0]
    spectrum = jnp.fft.rfft(signal, n=length, axis=0) * jnp.fft.rfft(filt, n=length, axis=0)
    return jnp.fft.irfft(spectrum, n=length, axis=0)[: signal.shape[0]]


def lag_sums(later_part, earlier_part):
    length = 2 * later_part.shape[0]
    spectrum = jnp.fft.rfft(later_part, n=length, axis=0) * jnp.conj(jnp.fft.rfft(earlier_part, n=length, axis=0))
    return jnp.fft.irfft(spectrum, n=length, axis=0)[:TAPS]


def front_part(stream_block, short_block, long_block, gain_block):
    stream_f = stream_block.astype(jnp.float32)
    mixed = sum(short_block[j] * shift_down(stream_f, j) for j in range(SHORT))
    key_value = (mixed[:, 1] * mixed[:, 2]).astype(jnp.bfloat16)
    key_value_f = key_value.astype(jnp.float32)
    filtered = causal_long(key_value_f, long_block) + gain_block * key_value_f
    return stream_f, mixed, key_value_f, filtered


def forward_block(items):
    stream_block, short_block, long_block, gain_block, keep_block = items
    stream_f, mixed, key_value_f, filtered = front_part(stream_block, short_block, long_block, gain_block)
    return (mixed[:, 0] * filtered * keep_block).astype(jnp.bfloat16)


def backward_block(items):
    stream_block, short_block, long_block, gain_block, grad_block = items
    stream_f, mixed, key_value_f, filtered = front_part(stream_block, short_block, long_block, gain_block)
    grad_query = grad_block * filtered
    grad_filt = lax.optimization_barrier((grad_block * mixed[:, 0]).astype(jnp.bfloat16)).astype(jnp.float32)
    grad_key_value = causal_long(grad_filt[::-1], long_block)[::-1] + gain_block * grad_filt
    grad_long = lag_sums(grad_filt, key_value_f)
    grad_gain = jnp.sum(grad_filt * key_value_f, axis=0)
    grad_mixed = jnp.stack([grad_query, grad_key_value * mixed[:, 2], grad_key_value * mixed[:, 1]], axis=1)
    grad_mixed = lax.optimization_barrier(grad_mixed.astype(jnp.bfloat16)).astype(jnp.float32)
    grad_stream = sum(short_block[j] * shift_up(grad_mixed, j) for j in range(SHORT)).astype(jnp.bfloat16)
    grad_short = jnp.stack([jnp.sum(grad_mixed * shift_down(stream_f, j), axis=0) for j in range(SHORT)])
    return grad_stream, grad_long, grad_short, grad_gain


def reference(proj_in, short_taps, long_taps, skip_gain, keep, w_out, grad_out):
    block_width = min(512, D)
    block_count = D // block_width
    streams = proj_in.reshape(TOKENS, 3, block_count, block_width).transpose(2, 0, 1, 3)
    shorts = short_taps.reshape(SHORT, 3, block_count, block_width).transpose(2, 0, 1, 3)
    longs = long_taps.reshape(TAPS, block_count, block_width).transpose(1, 0, 2)
    gains = skip_gain.reshape(block_count, block_width)
    keep_f = keep.astype(jnp.float32)
    keeps = keep_f.reshape(block_count, block_width)
    gated = lax.map(forward_block, (streams, shorts, longs, gains, keeps))
    gated = gated.transpose(1, 0, 2).reshape(TOKENS, D)
    total = jnp.zeros((TOKENS, DOUT), jnp.float32)
    for index in range(N_CHAN):
        lower = index * CHAN_BLOCK
        term = jnp.dot(gated[:, lower:lower + CHAN_BLOCK], w_out[lower:lower + CHAN_BLOCK], preferred_element_type=jnp.float32)
        total = total + lax.optimization_barrier(term.astype(jnp.bfloat16)).astype(jnp.float32)
    output = total.astype(jnp.bfloat16)
    grad_gated = jnp.dot(grad_out, w_out.T, preferred_element_type=jnp.float32) * keep_f
    grads = grad_gated.reshape(TOKENS, block_count, block_width).transpose(1, 0, 2)
    grad_stream, grad_long, grad_short, grad_gain = lax.map(backward_block, (streams, shorts, longs, gains, grads))
    grad_proj_in = grad_stream.transpose(1, 2, 0, 3).reshape(TOKENS, 3, D)
    grad_long_taps = grad_long.transpose(1, 0, 2).reshape(TAPS, D)
    grad_short_taps = grad_short.transpose(1, 2, 0, 3).reshape(SHORT, 3, D)
    grad_skip_gain = grad_gain.reshape(D)
    return output, grad_proj_in, grad_long_taps, grad_short_taps, grad_skip_gain
```

```python
import functools

import jax
import jax.numpy as jnp
import numpy as np
from jax import lax
from jax.experimental import pallas as pl
from jax.experimental.pallas import tpu as pltpu
from jax.sharding import PartitionSpec as P

GROUP = 16
EDGE = 8
CHUNKS = 4
F32 = jnp.float32
BF16 = jnp.bfloat16


def shifted(x, axis, by):
    peers = lax.axis_size(axis)
    pairs = [(i, i + by) for i in range(peers) if 0 <= i + by < peers]
    return lax.ppermute(x, axis, pairs)


def spectral(tokens, taps):
    length = tokens + taps
    freq = np.arange(length // 2) + 0.5
    angle = 2 * np.pi * freq[:, None] * np.arange(length)[None, :] / length
    return np.concatenate([np.cos(angle), -np.sin(angle)], axis=0)


def dot(a, b):
    return jnp.dot(a, b, preferred_element_type=F32)


def dot_nt(a, b):
    return lax.dot_general(a, b, (((1,), (1,)), ((), ())), preferred_element_type=F32)


def product(x, h, half):
    xr, xi, hr, hi = x[:half], x[half:], h[:half], h[half:]
    return jnp.concatenate([xr * hr - xi * hi, xr * hi + xi * hr], axis=0)


def product_conj(x, h, half):
    xr, xi, hr, hi = x[:half], x[half:], h[:half], h[half:]
    return jnp.concatenate([xr * hr + xi * hi, xi * hr - xr * hi], axis=0)


def selector(slot_row, wide):
    rows = lax.broadcasted_iota(jnp.int32, (wide // 2, wide), 0)
    return jnp.where(rows == slot_row, 1.0, 0.0).astype(BF16)


def pack_kernel(slot_ref, w_ref, out_ref):
    wide = w_ref.shape[0]
    out_ref[...] = dot(selector(slot_ref[0:1, :], wide), w_ref[...]).astype(BF16)


def mix_kernel(x_ref, edge_ref, short_ref, mixed_ref, kv_ref, pad):
    tokens = x_ref.shape[1]
    taps = short_ref.shape[1]
    for i in range(3):
        pad[0:EDGE, :] = edge_ref[i].astype(F32)
        pad[EDGE:, :] = x_ref[i].astype(F32)
        total = short_ref[i, 0:1, :] * pad[EDGE : EDGE + tokens, :]
        for j in range(1, taps):
            total += short_ref[i, j : j + 1, :] * pad[EDGE - j : EDGE - j + tokens, :]
        mixed_ref[i] = total
    kv_ref[...] = (mixed_ref[1] * mixed_ref[2]).astype(BF16)


def forward_kernel(
    own_ref, next_ref, inv_ref, kv_ref, before_ref, q_ref, long_ref, gain_ref, slot_ref,
    filtered_ref, gated_ref, kspec_ref, hspec_ref,
):
    half = own_ref.shape[0] // 2
    taps = long_ref.shape[0]
    wide = kv_ref.shape[1]
    kv = kv_ref[...]
    kspec = dot(own_ref[...], kv) - dot(next_ref[...], before_ref[...])
    hspec = dot(own_ref[:, :taps], long_ref[...].astype(BF16))
    spec = product(kspec, hspec, half)
    filtered = dot(inv_ref[...], spec.astype(BF16)) + gain_ref[0:1, :] * kv.astype(F32)
    filtered_ref[...] = filtered
    gated = (q_ref[0] * filtered).astype(BF16)
    gated_ref[...] = dot_nt(gated, selector(slot_ref[0:1, :], wide)).astype(BF16)
    kspec_ref[...] = kspec.astype(BF16)
    hspec_ref[...] = hspec.astype(BF16)


def grad_kernel(
    own_ref, inv_ref, panel_ref, go_ref, gated_ref, slot_ref, filtered_ref, q_ref, kv_ref, kspec_ref,
    out_ref, gq_ref, gf_ref, sums_ref,
):
    half = own_ref.shape[0] // 2
    taps = sums_ref.shape[0] - EDGE
    wide = kv_ref.shape[1]
    panel = panel_ref[...]

    @pl.when(pl.program_id(0) == 0)
    def _():
        out_ref[...] = jnp.zeros_like(out_ref)

    out_ref[...] += dot(gated_ref[...], panel)
    gi = dot_nt(go_ref[...], panel)
    gi_high = gi.astype(BF16)
    gi_low = (gi - gi_high.astype(F32)).astype(BF16)
    pick = selector(slot_ref[0:1, :], wide)
    gg = dot(gi_high, pick) + dot(gi_low, pick)
    gq_ref[...] = (gg * filtered_ref[...]).astype(BF16)
    gf = (gg * q_ref[0]).astype(BF16)
    gf_ref[...] = gf
    spec = product_conj(dot(own_ref[...], gf), kspec_ref[...].astype(F32), half)
    sums_ref[:taps, :] = dot(inv_ref[:taps, :], spec.astype(BF16))
    gain = jnp.sum(gf.astype(F32) * kv_ref[...].astype(F32), axis=0, keepdims=True)
    sums_ref[taps:, :] = jnp.broadcast_to(gain, (EDGE, wide))


def back_kernel(
    own_ref, next_ref, inv_ref, gf_ref, after_ref, hspec_ref, gain_ref, gq_ref, k_ref, v_ref, x_ref, edge_ref, short_ref,
    gp_ref, tail_ref, head_ref, gs_ref, pad, pad_x,
):
    half = own_ref.shape[0] // 2
    tokens = x_ref.shape[1]
    taps = short_ref.shape[1]
    gf = gf_ref[...]
    gspec = dot(own_ref[...], gf) + dot(next_ref[...], after_ref[...])
    spec = product_conj(gspec, hspec_ref[...].astype(F32), half)
    gkv = dot(inv_ref[...], spec.astype(BF16)) + gain_ref[0:1, :] * gf.astype(F32)
    grads = (
        gq_ref[...],
        (gkv * v_ref[0]).astype(BF16),
        (gkv * k_ref[0]).astype(BF16),
    )
    pad[tokens:, :] = jnp.zeros((EDGE, gf.shape[1]), F32)
    for i in range(3):
        gm = grads[i]
        tail_ref[i] = gm[tokens - 2 * EDGE :, :]
        head_ref[i] = gm[: 2 * EDGE, :]
        gmf = gm.astype(F32)
        pad[:tokens, :] = gmf
        pad_x[0:EDGE, :] = edge_ref[i].astype(F32)
        pad_x[EDGE:, :] = x_ref[i].astype(F32)
        total = short_ref[i, 0:1, :] * gmf
        gs_ref[i, 0:1, :] = jnp.sum(gmf * pad_x[EDGE:, :], axis=0, keepdims=True)
        for j in range(1, taps):
            total += short_ref[i, j : j + 1, :] * pad[j : j + tokens, :]
            gs_ref[i, j : j + 1, :] = jnp.sum(
                pad[:tokens, :] * pad_x[EDGE - j : EDGE - j + tokens, :], axis=0, keepdims=True
            )
        gs_ref[i, taps:, :] = jnp.zeros((EDGE - taps, gf.shape[1]), F32)
        gp_ref[i] = total.astype(BF16)


def tail_kernel(tail_ref, after_ref, short_ref, gp_ref, out_ref, pad):
    del gp_ref
    rows = tail_ref.shape[1]
    taps = short_ref.shape[1]
    for i in range(3):
        pad[:rows, :] = tail_ref[i].astype(F32)
        pad[rows:, :] = after_ref[i].astype(F32)
        total = short_ref[i, 0:1, :] * pad[:rows, :]
        for j in range(1, taps):
            total += short_ref[i, j : j + 1, :] * pad[j : j + rows, :]
        out_ref[i] = total.astype(BF16)


def params(flops=0, moved=0):
    return dict(
        compiler_params=pltpu.CompilerParams(
            dimension_semantics=("arbitrary",), vmem_limit_bytes=56 * 2**20
        ),
        cost_estimate=pl.CostEstimate(flops=flops, bytes_accessed=moved, transcendentals=0),
    )


def local(proj_in, short_taps, long_taps, skip_gain, keep, w_out, grad_out):
    tokens, _, channels = proj_in.shape
    tap_count = long_taps.shape[0]
    short_len = short_taps.shape[0]
    size = tokens + tap_count
    chunks = CHUNKS if channels % (CHUNKS * 512) == 0 else 1
    width = channels // chunks
    block = min(512, width)
    steps = width // block

    matrix = spectral(tokens, tap_count)
    own = jnp.asarray(matrix[:, :tokens], BF16)
    nxt = jnp.asarray(matrix[:, tokens:], BF16)
    inv = jnp.asarray(matrix[:, :tokens].T * (2.0 / size), BF16)

    x = proj_in.transpose(1, 0, 2)
    short = short_taps.transpose(1, 0, 2)
    gain = jnp.broadcast_to(skip_gain[None], (EDGE, channels))
    groups = keep.reshape(channels // GROUP, GROUP)
    rank = jnp.cumsum(groups, axis=1) - 1
    base = (jnp.arange(channels // GROUP, dtype=jnp.int32) % (block // GROUP)) * (GROUP // 2)
    slot = jnp.where(groups == 1, rank + base[:, None], -1).reshape(1, channels)
    slot = jnp.broadcast_to(slot, (EDGE, channels))
    go = lax.all_gather(grad_out, "chan", axis=1, tiled=True)
    features = w_out.shape[1]
    whole = pl.BlockSpec(memory_space=pltpu.VMEM)

    def two(rows, off=0, wide=block):
        return pl.BlockSpec((rows, wide), lambda c: (0, c + off))

    def three(lead, rows, off=0, at=0):
        return pl.BlockSpec((lead, rows, block), lambda c: (at, 0, c + off))

    def shape2(rows, kind, wide=width):
        return jax.ShapeDtypeStruct((rows, wide), kind)

    def shape3(lead, rows, kind):
        return jax.ShapeDtypeStruct((lead, rows, width), kind)

    panels = []
    for n in range(chunks):
        off = n * steps
        rows = pl.pallas_call(
            pack_kernel,
            grid=(steps,),
            in_specs=[two(EDGE, off), pl.BlockSpec((block, features), lambda c, off=off: (c + off, 0))],
            out_specs=pl.BlockSpec((block // 2, features), lambda c: (c, 0)),
            out_shape=jax.ShapeDtypeStruct((width // 2, features), BF16),
            name=f"pack{n}",
            **params(width * block * features, 3 * width * features),
        )(slot, w_out)
        panels.append(lax.all_gather(rows, "seq", axis=1, tiled=True))

    edge = shifted(x[:, tokens - EDGE :, :], "seq", 1)
    front = []
    for n in range(chunks):
        off = n * steps
        mixed, kv = pl.pallas_call(
            mix_kernel,
            grid=(steps,),
            in_specs=[three(3, tokens, off), three(3, EDGE, off), three(3, short_len, off)],
            out_specs=[three(3, tokens), two(tokens)],
            out_shape=[shape3(3, tokens, F32), shape2(tokens, BF16)],
            scratch_shapes=[pltpu.VMEM((tokens + EDGE, block), F32)],
            name=f"mix{n}",
            **params(42 * tokens * width, 20 * tokens * width),
        )(x, edge, short)
        before = shifted(kv[tokens - tap_count :], "seq", 1)
        front.append((mixed, kv, before))

    forward = []
    for n in range(chunks):
        off = n * steps
        mixed, kv, before = front[n]
        forward.append(
            pl.pallas_call(
                forward_kernel,
                grid=(steps,),
                in_specs=[
                    whole, whole, whole, two(tokens), two(tap_count), three(1, tokens),
                    two(tap_count, off), two(EDGE, off), two(EDGE, off),
                ],
                out_specs=[two(tokens), two(tokens, 0, block // 2), two(size), two(size)],
                out_shape=[
                    shape2(tokens, F32),
                    shape2(tokens, BF16, width // 2),
                    shape2(size, BF16),
                    shape2(size, BF16),
                ],
                name=f"forward{n}",
                **params(8 * size * tokens * width, 20 * tokens * width),
            )(own, nxt, inv, kv, before, mixed, long_taps, gain, slot)
        )

    totals, grads = None, []
    for n in range(chunks):
        off = n * steps
        mixed, kv, _ = front[n]
        filtered, gated, kspec, hspec = forward[n]
        out_wide = panels[n].shape[1]
        part, gq, gf, sums = pl.pallas_call(
            grad_kernel,
            grid=(steps,),
            in_specs=[
                whole, whole, pl.BlockSpec((block // 2, out_wide), lambda c: (c, 0)), whole,
                two(tokens, 0, block // 2), two(EDGE, off), two(tokens), three(1, tokens), two(tokens), two(size),
            ],
            out_specs=[pl.BlockSpec((tokens, out_wide), lambda c: (0, 0)), two(tokens), two(tokens), two(tap_count + EDGE)],
            out_shape=[
                jax.ShapeDtypeStruct((tokens, out_wide), F32),
                shape2(tokens, BF16), shape2(tokens, BF16), shape2(tap_count + EDGE, F32),
            ],
            name=f"grad{n}",
            **params(2 * tokens * width * out_wide, width * out_wide),
        )(own, inv, panels[n], go, gated, slot, filtered, mixed, kv, kspec)
        totals = part if totals is None else totals + part
        after = shifted(gf[:tap_count], "seq", -1)
        gp, tail, head, gs = pl.pallas_call(
            back_kernel,
            grid=(steps,),
            in_specs=[
                whole, whole, whole, two(tokens), two(tap_count), two(size), two(EDGE, off), two(tokens),
                three(1, tokens, 0, 1), three(1, tokens, 0, 2),
                three(3, tokens, off), three(3, EDGE, off), three(3, short_len, off),
            ],
            out_specs=[three(3, tokens), three(3, 2 * EDGE), three(3, 2 * EDGE), three(3, EDGE)],
            out_shape=[
                shape3(3, tokens, BF16), shape3(3, 2 * EDGE, BF16), shape3(3, 2 * EDGE, BF16), shape3(3, EDGE, F32),
            ],
            scratch_shapes=[pltpu.VMEM((tokens + EDGE, block), F32)] * 2,
            name=f"back{n}",
            **params(8 * size * tokens * width, 30 * tokens * width),
        )(own, nxt, inv, gf, after, hspec, gain, gq, mixed, mixed, x, edge, short)
        grads.append((gp, tail, head, gs, sums))

    def joined(k, axis):
        return jnp.concatenate([g[k] for g in grads], axis=axis) if chunks > 1 else grads[0][k]

    summed = lax.psum_scatter(totals.astype(BF16), "chan", scatter_dimension=1, tiled=True)
    output = summed.astype(F32).astype(BF16)
    gp, tail, head = joined(0, 2), joined(1, 2), joined(2, 2)
    after = shifted(head[:, :EDGE], "seq", -1)
    grad_proj = pl.pallas_call(
        tail_kernel,
        grid=(channels // block,),
        in_specs=[
            three(3, 2 * EDGE), three(3, EDGE), three(3, short_len), pl.BlockSpec(memory_space=pl.ANY),
        ],
        out_specs=pl.BlockSpec((3, 2 * EDGE, block), lambda c: (0, tokens // (2 * EDGE) - 1, c)),
        out_shape=jax.ShapeDtypeStruct((3, tokens, channels), BF16),
        scratch_shapes=[pltpu.VMEM((3 * EDGE, block), F32)],
        input_output_aliases={3: 0},
        name="tail",
        **params(42 * 16 * channels, 300 * channels),
    )(tail, after, short, gp)
    sums, gs = lax.psum((joined(4, 1), joined(3, 2)), "seq")
    return (
        output,
        grad_proj.transpose(1, 0, 2),
        sums[:tap_count],
        gs[:, :short_len].transpose(1, 0, 2),
        sums[tap_count],
    )


def solution(mesh):
    placed = (
        P("seq", None, "chan"),
        P(None, None, "chan"),
        P(None, "chan"),
        P("chan"),
        P("chan"),
        P("chan", "seq"),
        P("seq", "chan"),
    )
    return jax.shard_map(
        local,
        mesh=mesh,
        in_specs=placed,
        out_specs=(
            P("seq", "chan"),
            P("seq", None, "chan"),
            P(None, "chan"),
            P(None, None, "chan"),
            P("chan"),
        ),
        check_vma=False,
    )
```

```python
import functools

import jax
import jax.numpy as jnp
import numpy as np
from jax import lax
from jax.experimental import pallas as pl
from jax.experimental.pallas import tpu as pltpu
from jax.sharding import PartitionSpec as P

GROUP = 16
EDGE = 8
CHUNKS = 4
F32 = jnp.float32
BF16 = jnp.bfloat16


def shifted(x, axis, by):
    peers = lax.axis_size(axis)
    pairs = [(i, i + by) for i in range(peers) if 0 <= i + by < peers]
    return lax.ppermute(x, axis, pairs)


def tree_sum(parts, axis):
    peers = lax.axis_size(axis)
    if peers & (peers - 1) or parts.shape[0] % peers:
        return lax.psum(parts, axis)
    me = lax.axis_index(axis)
    bits = [1 << s for s in range(peers.bit_length() - 1)]
    for bit in bits:
        half = parts.shape[0] // 2
        upper = (me & bit) != 0
        low, high = parts[:half], parts[half:]
        pairs = [(i, i ^ bit) for i in range(peers)]
        got = lax.ppermute(jnp.where(upper, low, high), axis, pairs)
        parts = jnp.where(upper, high, low) + got
    for bit in reversed(bits):
        upper = (me & bit) != 0
        pairs = [(i, i ^ bit) for i in range(peers)]
        got = lax.ppermute(parts, axis, pairs)
        parts = jnp.concatenate([jnp.where(upper, got, parts), jnp.where(upper, parts, got)], axis=0)
    return parts


def spectral(tokens, taps):
    length = tokens + taps
    freq = np.arange(length // 2) + 0.5
    angle = 2 * np.pi * freq[:, None] * np.arange(length)[None, :] / length
    return np.concatenate([np.cos(angle), -np.sin(angle)], axis=0)


def dot(a, b):
    return jnp.dot(a, b, preferred_element_type=F32)


def dot_nt(a, b):
    return lax.dot_general(a, b, (((1,), (1,)), ((), ())), preferred_element_type=F32)


def product(x, h, half):
    xr, xi, hr, hi = x[:half], x[half:], h[:half], h[half:]
    return jnp.concatenate([xr * hr - xi * hi, xr * hi + xi * hr], axis=0)


def product_conj(x, h, half):
    xr, xi, hr, hi = x[:half], x[half:], h[:half], h[half:]
    return jnp.concatenate([xr * hr + xi * hi, xi * hr - xr * hi], axis=0)


def selector(slot_row, wide):
    rows = lax.broadcasted_iota(jnp.int32, (wide // 2, wide), 0)
    return jnp.where(rows == slot_row, 1.0, 0.0).astype(BF16)


def pack_kernel(slot_ref, w_ref, out_ref):
    wide = w_ref.shape[0]
    out_ref[...] = dot(selector(slot_ref[0:1, :], wide), w_ref[...]).astype(BF16)


def mix_kernel(x_ref, edge_ref, short_ref, mixed_ref, kv_ref, pad):
    tokens = x_ref.shape[1]
    taps = short_ref.shape[1]
    for i in range(3):
        pad[0:EDGE, :] = edge_ref[i].astype(F32)
        pad[EDGE:, :] = x_ref[i].astype(F32)
        total = short_ref[i, 0:1, :] * pad[EDGE : EDGE + tokens, :]
        for j in range(1, taps):
            total += short_ref[i, j : j + 1, :] * pad[EDGE - j : EDGE - j + tokens, :]
        mixed_ref[i] = total
    kv_ref[...] = (mixed_ref[1] * mixed_ref[2]).astype(BF16)


def forward_kernel(
    own_ref, next_ref, inv_ref, kv_ref, before_ref, q_ref, long_ref, gain_ref, slot_ref,
    filtered_ref, gated_ref, kspec_ref, hspec_ref,
):
    half = own_ref.shape[0] // 2
    taps = long_ref.shape[0]
    wide = kv_ref.shape[1]
    kv = kv_ref[...]
    kspec = dot(own_ref[...], kv) - dot(next_ref[...], before_ref[...])
    hspec = dot(own_ref[:, :taps], long_ref[...].astype(BF16))
    spec = product(kspec, hspec, half)
    filtered = dot(inv_ref[...], spec.astype(BF16)) + gain_ref[0:1, :] * kv.astype(F32)
    filtered_ref[...] = filtered
    gated = (q_ref[0] * filtered).astype(BF16)
    gated_ref[...] = dot_nt(gated, selector(slot_ref[0:1, :], wide)).astype(BF16)
    kspec_ref[...] = kspec.astype(BF16)
    hspec_ref[...] = hspec.astype(BF16)


def grad_kernel(
    own_ref, inv_ref, panel_ref, go_ref, gated_ref, slot_ref, filtered_ref, q_ref, kv_ref, kspec_ref,
    out_ref, gq_ref, gf_ref, sums_ref,
):
    half = own_ref.shape[0] // 2
    taps = sums_ref.shape[0] - 2 * EDGE
    wide = kv_ref.shape[1]
    panel = panel_ref[...]

    @pl.when(pl.program_id(0) == 0)
    def _():
        out_ref[...] = jnp.zeros_like(out_ref)

    out_ref[...] += dot(gated_ref[...], panel)
    gi = dot_nt(go_ref[...], panel)
    gi_high = gi.astype(BF16)
    gi_low = (gi - gi_high.astype(F32)).astype(BF16)
    pick = selector(slot_ref[0:1, :], wide)
    gg = dot(gi_high, pick) + dot(gi_low, pick)
    gq_ref[...] = (gg * filtered_ref[...]).astype(BF16)
    gf = (gg * q_ref[0]).astype(BF16)
    gf_ref[...] = gf
    spec = product_conj(dot(own_ref[...], gf), kspec_ref[...].astype(F32), half)
    sums_ref[:taps, :] = dot(inv_ref[:taps, :], spec.astype(BF16)).astype(BF16)
    gain = jnp.sum(gf.astype(F32) * kv_ref[...].astype(F32), axis=0, keepdims=True)
    sums_ref[taps:, :] = jnp.broadcast_to(gain, (2 * EDGE, wide)).astype(BF16)


def back_kernel(
    own_ref, next_ref, inv_ref, gf_ref, after_ref, hspec_ref, gain_ref, gq_ref, k_ref, v_ref, x_ref, edge_ref, short_ref,
    gp_ref, tail_ref, head_ref, gs_ref, pad, pad_x,
):
    half = own_ref.shape[0] // 2
    tokens = x_ref.shape[1]
    taps = short_ref.shape[1]
    gf = gf_ref[...]
    gspec = dot(own_ref[...], gf) + dot(next_ref[...], after_ref[...])
    spec = product_conj(gspec, hspec_ref[...].astype(F32), half)
    gkv = dot(inv_ref[...], spec.astype(BF16)) + gain_ref[0:1, :] * gf.astype(F32)
    grads = (
        gq_ref[...],
        (gkv * v_ref[0]).astype(BF16),
        (gkv * k_ref[0]).astype(BF16),
    )
    pad[tokens:, :] = jnp.zeros((EDGE, gf.shape[1]), F32)
    pieces, _, lanes = gs_ref.shape
    gs_ref[...] = jnp.zeros_like(gs_ref)

    def put(row, value):
        for b in range(pieces):
            gs_ref[b, row : row + 1, :] = value[:, b * lanes : (b + 1) * lanes]

    for i in range(3):
        gm = grads[i]
        tail_ref[i] = gm[tokens - 2 * EDGE :, :]
        head_ref[i] = gm[: 2 * EDGE, :]
        gmf = gm.astype(F32)
        pad[:tokens, :] = gmf
        pad_x[0:EDGE, :] = edge_ref[i].astype(F32)
        pad_x[EDGE:, :] = x_ref[i].astype(F32)
        total = short_ref[i, 0:1, :] * gmf
        put(i * EDGE, jnp.sum(gmf * pad_x[EDGE:, :], axis=0, keepdims=True))
        for j in range(1, taps):
            total += short_ref[i, j : j + 1, :] * pad[j : j + tokens, :]
            lagged = gmf * pad_x[EDGE - j : EDGE - j + tokens, :]
            put(i * EDGE + j, jnp.sum(lagged, axis=0, keepdims=True))
        gp_ref[i] = total.astype(BF16)


def tail_kernel(tail_ref, after_ref, short_ref, gp_ref, out_ref, pad):
    del gp_ref
    rows = tail_ref.shape[1]
    taps = short_ref.shape[1]
    for i in range(3):
        pad[:rows, :] = tail_ref[i].astype(F32)
        pad[rows:, :] = after_ref[i].astype(F32)
        total = short_ref[i, 0:1, :] * pad[:rows, :]
        for j in range(1, taps):
            total += short_ref[i, j : j + 1, :] * pad[j : j + rows, :]
        out_ref[i] = total.astype(BF16)


def params(flops=0, moved=0):
    return dict(
        compiler_params=pltpu.CompilerParams(
            dimension_semantics=("arbitrary",), vmem_limit_bytes=56 * 2**20
        ),
        cost_estimate=pl.CostEstimate(flops=flops, bytes_accessed=moved, transcendentals=0),
    )


def local(proj_in, short_taps, long_taps, skip_gain, keep, w_out, grad_out):
    tokens, _, channels = proj_in.shape
    tap_count = long_taps.shape[0]
    short_len = short_taps.shape[0]
    size = tokens + tap_count
    chunks = CHUNKS if channels % (CHUNKS * 512) == 0 else 1
    width = channels // chunks
    block = min(512, width)
    lanes = min(256, block)
    steps = width // block

    matrix = spectral(tokens, tap_count)
    own = jnp.asarray(matrix[:, :tokens], BF16)
    nxt = jnp.asarray(matrix[:, tokens:], BF16)
    inv = jnp.asarray(matrix[:, :tokens].T * (2.0 / size), BF16)

    x = proj_in.transpose(1, 0, 2)
    short = short_taps.transpose(1, 0, 2)
    gain = jnp.broadcast_to(skip_gain[None], (EDGE, channels))
    groups = keep.reshape(channels // GROUP, GROUP)
    rank = jnp.cumsum(groups, axis=1) - 1
    base = (jnp.arange(channels // GROUP, dtype=jnp.int32) % (block // GROUP)) * (GROUP // 2)
    slot = jnp.where(groups == 1, rank + base[:, None], -1).reshape(1, channels)
    slot = jnp.broadcast_to(slot, (EDGE, channels))
    go = lax.all_gather(grad_out, "chan", axis=1, tiled=True)
    features = w_out.shape[1]
    whole = pl.BlockSpec(memory_space=pltpu.VMEM)

    def two(rows, off=0, wide=block):
        return pl.BlockSpec((rows, wide), lambda c: (0, c + off))

    def three(lead, rows, off=0, at=0):
        return pl.BlockSpec((lead, rows, block), lambda c: (at, 0, c + off))

    def shape2(rows, kind, wide=width):
        return jax.ShapeDtypeStruct((rows, wide), kind)

    def shape3(lead, rows, kind):
        return jax.ShapeDtypeStruct((lead, rows, width), kind)

    packed = pl.pallas_call(
        pack_kernel,
        grid=(channels // block,),
        in_specs=[two(EDGE), pl.BlockSpec((block, features), lambda c: (c, 0))],
        out_specs=pl.BlockSpec((block // 2, features), lambda c: (c, 0)),
        out_shape=jax.ShapeDtypeStruct((channels // 2, features), BF16),
        name="pack",
        **params(channels * block * features, 3 * channels * features),
    )(slot, w_out)
    panel = lax.all_gather(packed, "seq", axis=1, tiled=True)

    edge = shifted(x[:, tokens - EDGE :, :], "seq", 1)
    front = []
    for n in range(chunks):
        off = n * steps
        mixed, kv = pl.pallas_call(
            mix_kernel,
            grid=(steps,),
            in_specs=[three(3, tokens, off), three(3, EDGE, off), three(3, short_len, off)],
            out_specs=[three(3, tokens), two(tokens)],
            out_shape=[shape3(3, tokens, F32), shape2(tokens, BF16)],
            scratch_shapes=[pltpu.VMEM((tokens + EDGE, block), F32)],
            name=f"mix{n}",
            **params(42 * tokens * width, 20 * tokens * width),
        )(x, edge, short)
        before = shifted(kv[tokens - tap_count :], "seq", 1)
        front.append((mixed, kv, before))

    forward = []
    for n in range(chunks):
        off = n * steps
        mixed, kv, before = front[n]
        forward.append(
            pl.pallas_call(
                forward_kernel,
                grid=(steps,),
                in_specs=[
                    whole, whole, whole, two(tokens), two(tap_count), three(1, tokens),
                    two(tap_count, off), two(EDGE, off), two(EDGE, off),
                ],
                out_specs=[two(tokens), two(tokens, 0, block // 2), two(size), two(size)],
                out_shape=[
                    shape2(tokens, F32),
                    shape2(tokens, BF16, width // 2),
                    shape2(size, BF16),
                    shape2(size, BF16),
                ],
                name=f"forward{n}",
                **params(8 * size * tokens * width, 20 * tokens * width),
            )(own, nxt, inv, kv, before, mixed, long_taps, gain, slot)
        )

    totals, middle, grads = None, [], []
    for n in range(chunks):
        off = n * steps
        mixed, kv, _ = front[n]
        filtered, gated, kspec, hspec = forward[n]
        out_wide = panel.shape[1]
        part, gq, gf, sums = pl.pallas_call(
            grad_kernel,
            grid=(steps,),
            in_specs=[
                whole, whole, pl.BlockSpec((block // 2, out_wide), lambda c, off=off: (c + off, 0)), whole,
                two(tokens, 0, block // 2), two(EDGE, off), two(tokens), three(1, tokens), two(tokens), two(size),
            ],
            out_specs=[pl.BlockSpec((tokens, out_wide), lambda c: (0, 0)), two(tokens), two(tokens), two(tap_count + 2 * EDGE)],
            out_shape=[
                jax.ShapeDtypeStruct((tokens, out_wide), F32),
                shape2(tokens, BF16), shape2(tokens, BF16), shape2(tap_count + 2 * EDGE, BF16),
            ],
            name=f"grad{n}",
            **params(2 * tokens * width * out_wide, width * out_wide),
        )(own, inv, panel, go, gated, slot, filtered, mixed, kv, kspec)
        totals = part if totals is None else totals + part
        middle.append((gq, gf, sums))
    long_sum = lax.psum(jnp.concatenate([m[2] for m in middle], axis=1), "seq").astype(F32)
    summed = lax.psum_scatter(totals.astype(BF16), "chan", scatter_dimension=1, tiled=True)
    output = summed.astype(F32).astype(BF16)
    for n in range(chunks):
        off = n * steps
        mixed = front[n][0]
        hspec = forward[n][3]
        gq, gf, _ = middle[n]
        after = shifted(gf[:tap_count], "seq", -1)
        gp, tail, head, gs = pl.pallas_call(
            back_kernel,
            grid=(steps,),
            in_specs=[
                whole, whole, whole, two(tokens), two(tap_count), two(size), two(EDGE, off), two(tokens),
                three(1, tokens, 0, 1), three(1, tokens, 0, 2),
                three(3, tokens, off), three(3, EDGE, off), three(3, short_len, off),
            ],
            out_specs=[three(3, tokens), three(3, 2 * EDGE), three(3, 2 * EDGE),
                pl.BlockSpec((block // lanes, 3 * EDGE, lanes), lambda c: (c, 0, 0)),
            ],
            out_shape=[
                shape3(3, tokens, BF16), shape3(3, 2 * EDGE, BF16), shape3(3, 2 * EDGE, BF16),
                jax.ShapeDtypeStruct((width // lanes, 3 * EDGE, lanes), F32),
            ],
            scratch_shapes=[pltpu.VMEM((tokens + EDGE, block), F32)] * 2,
            name=f"back{n}",
            **params(8 * size * tokens * width, 30 * tokens * width),
        )(own, nxt, inv, gf, after, hspec, gain, gq, mixed, mixed, x, edge, short)
        grads.append((gp, tail, head, gs))

    def joined(k, axis):
        return jnp.concatenate([g[k] for g in grads], axis=axis) if chunks > 1 else grads[0][k]

    gp, tail, head = joined(0, 2), joined(1, 2), joined(2, 2)
    after = shifted(head[:, :EDGE], "seq", -1)
    grad_proj = pl.pallas_call(
        tail_kernel,
        grid=(channels // block,),
        in_specs=[
            three(3, 2 * EDGE), three(3, EDGE), three(3, short_len), pl.BlockSpec(memory_space=pl.ANY),
        ],
        out_specs=pl.BlockSpec((3, 2 * EDGE, block), lambda c: (0, tokens // (2 * EDGE) - 1, c)),
        out_shape=jax.ShapeDtypeStruct((3, tokens, channels), BF16),
        scratch_shapes=[pltpu.VMEM((3 * EDGE, block), F32)],
        input_output_aliases={3: 0},
        name="tail",
        **params(42 * 16 * channels, 300 * channels),
    )(tail, after, short, gp)
    gs = tree_sum(joined(3, 0), "seq").transpose(1, 0, 2).reshape(3, EDGE, channels)
    return (
        output,
        grad_proj.transpose(1, 0, 2),
        long_sum[:tap_count],
        gs[:, :short_len].transpose(1, 0, 2),
        long_sum[tap_count],
    )


def solution(mesh):
    placed = (
        P("seq", None, "chan"),
        P(None, None, "chan"),
        P(None, "chan"),
        P("chan"),
        P("chan"),
        P("chan", "seq"),
        P("seq", "chan"),
    )
    return jax.shard_map(
        local,
        mesh=mesh,
        in_specs=placed,
        out_specs=(
            P("seq", "chan"),
            P("seq", None, "chan"),
            P(None, "chan"),
            P(None, None, "chan"),
            P("chan"),
        ),
        check_vma=False,
    )
```
